32 devices in a mesh: section: 2 (over x), dp: 4 (over z), mp: 4 (over y, core).
Axes of the slice: x: 2, y: 2, z: 4, core: 2. Of those that a mesh axis runs over, the one named last changes fastest.
Arguments:
- block_input: bfloat16 [4, 512, 768], P('dp', 'mp'), may hold values from -6 to 6
- out_cotangent: bfloat16 [4, 512, 768], P('dp', 'mp'), may hold values from -6 to 6
- segments: int32 [4, 512], P('dp'), may hold values from 0 to 7, never falling along the last dimension, each value on 1 to 128 neighbouring positions
- qkv_weight: bfloat16 [2, 768, 3, 768], P('section', 'dp', None, 'mp'), may hold values from -0.21875 to 0.21875
- out_weight: bfloat16 [2, 768, 768], P('section', 'mp', 'dp'), may hold values from -0.625 to 0.625
- up_weight: bfloat16 [2, 768, 3072], P('section', 'dp', 'mp'), may hold values from -0.21875 to 0.21875
- down_weight: bfloat16 [2, 3072, 768], P('section', 'mp', 'dp'), may hold values from -0.109375 to 0.109375
- vectors: float32 [2, 9984], P('section', ('dp', 'mp')), may hold values from 0.25 to 1.75
Outputs:
- layer_out: bfloat16 [2, 4, 512, 768], P('section', 'dp', 'mp')
- input_grad: bfloat16 [2, 4, 512, 768], P('section', 'dp', 'mp')
- qkv_grad: float32 [2, 768, 3, 768], P('section', 'dp', None, 'mp')
- out_grad: float32 [2, 768, 768], P('section', 'mp', 'dp')
- up_grad: float32 [2, 768, 3072], P('section', 'dp', 'mp')
- down_grad: float32 [2, 3072, 768], P('section', 'mp', 'dp')
- vector_grad: float32 [2, 9984], P('section', ('dp', 'mp'))
The draws below stay inside these ranges and needn't reach their ends.
Inputs may be any that keep to these rules, and one draw needn't show every extreme that they name: `segments`: document numbers never fall along a sequence; every document has 1 to 128 tokens and one has exactly 128.
All inputs are finite; a program needn't handle non-finite values.
Results may differ from the reference program's by a relative error of at most 0.02.
Values may be sent and summed in bfloat16 or wider, within the bound.
No kernel may reach another device: no remote copies, remote signals or barrier semaphores. Data moves between devices by JAX's collectives and lax.ppermute only.
A program may use at most 128 MiB of HBM per device.

```python
import math
import jax
import jax.numpy as jnp
import numpy as np
from jax import lax

D = 768
HEADS = 12
HD = 64
FF = 3072
ROT = 16
LEN = 512
SEGS = 8
SEG_MOST = 128
SEQS = 4
SECTIONS = 2
NV = 9984


def shard_levels(own_key, shape, shards, smallest, largest):
    def one(position, shards_of):
        draws = jax.random.uniform(jax.random.fold_in(jax.random.fold_in(own_key, 6), position), (shards_of,), jnp.float32, smallest / len(shards), largest / len(shards))
        return jnp.repeat(jnp.exp(draws), shape[position] // shards_of).reshape((-1,) + (1,) * (len(shape) - position - 1))

    loudness = one(*shards[0])
    for cut in shards[1:]:
        loudness = loudness * one(*cut)
    return loudness


def length_profile(number_of, total, most, lean):
    portions = [(1 << 20) // math.isqrt(standing ** lean) + 1 for standing in range(2, number_of + 1)]
    spare, holding = total - most - (number_of - 1), [1] * (number_of - 1)
    while spare > 0:
        free = [i for i in range(number_of - 1) if holding[i] < most]
        mass, budget = sum([portions[i] for i in free]), spare
        for i in free:
            more = min(most - holding[i], max(1, budget * portions[i] // mass), spare)
            holding[i] = holding[i] + more
            spare = spare - more
    return np.array([most] + holding)


def ragged_sizes(rng, number_of, total, limit, lean):
    if number_of == 2:
        one = jax.random.randint(rng, (), max(1, total - limit), min(limit, total - 1) + 1)
        return jnp.stack([one, total - one])
    tallies = jnp.asarray(length_profile(number_of, total, limit, lean), jnp.int32)
    couples = (number_of - 1) // 2
    source_of, taker = tallies[1:1 + 2 * couples:2], tallies[2:2 + 2 * couples:2]
    margin = jnp.minimum(source_of - 1, limit - taker)
    passed = jax.random.randint(jax.random.fold_in(rng, 1), (couples,), 0, 1 << 20) % (margin + 1)
    tallies = tallies.at[1:1 + 2 * couples:2].set(source_of - passed).at[2:2 + 2 * couples:2].set(taker + passed)
    return tallies[jax.random.permutation(jax.random.fold_in(rng, 2), number_of)]


def scatter_about(key, shape, spread, most, split=(), kind=jnp.bfloat16):
    factor_of = shard_levels(key, shape, split, -0.22, 0.18) if split else 1.0
    array = jax.random.normal(key, shape, jnp.float32) * spread * factor_of
    return jnp.minimum(jnp.maximum(array, -most), most).astype(kind)


def setup_inputs(seed: int = 0) -> dict:
    key_of = jax.random.split(jax.random.key(seed), 9)
    block_input = scatter_about(key_of[0], (SEQS, LEN, D), 1.0, 6.0, ((0, 4), (1, 4)))
    out_cotangent = scatter_about(key_of[1], (SEQS, LEN, D), 1.0, 6.0, ((0, 4), (1, 4)))
    segments = jax.vmap(lambda own: jnp.searchsorted(jnp.cumsum(ragged_sizes(own, SEGS, LEN, SEG_MOST, 1)), jnp.arange(LEN), side="right"))(jax.random.split(key_of[2], SEQS)).reshape((SEQS, LEN)).astype(jnp.int32)
    qkv_weight = scatter_about(key_of[3], (SECTIONS, D, 3, D), D ** -0.5, 0.21875, ((0, 2), (1, 4), (3, 4)))
    out_weight = scatter_about(key_of[4], (SECTIONS, D, D), (D // 8) ** -0.5, 0.625, ((0, 2), (1, 4), (2, 4)))
    up_weight = scatter_about(key_of[5], (SECTIONS, D, FF), D ** -0.5, 0.21875, ((0, 2), (1, 4), (2, 4)))
    down_weight = scatter_about(key_of[6], (SECTIONS, FF, D), FF ** -0.5, 0.109375, ((0, 2), (1, 4), (2, 4)))
    vectors = jnp.clip(1.0 + 0.15 * jax.random.normal(key_of[7], (SECTIONS, NV), jnp.float32), 0.25, 1.75)
    return {"block_input": block_input, "out_cotangent": out_cotangent, "segments": segments, "qkv_weight": qkv_weight, "out_weight": out_weight, "up_weight": up_weight, "down_weight": down_weight, "vectors": vectors}


epsilon = 1e-05
inv_root_two = 0.7071067811865476
inv_root_two_pi = 0.3989422804014327
masked_score = -1e+30

def normalize(values):
    average = lax.optimization_barrier(jnp.mean(values, axis=-1, keepdims=True))
    centered = values - average
    variance = lax.optimization_barrier(jnp.mean(centered * centered, axis=-1, keepdims=True))
    scaling = lax.rsqrt(variance + epsilon)
    return (centered * scaling, scaling)

def gelu_value(pre_act):
    return pre_act * (0.5 * (1.0 + lax.erf(pre_act * inv_root_two)))

def gelu_slope(pre_act):
    cumulative = 0.5 * (1.0 + lax.erf(pre_act * inv_root_two))
    density = jnp.exp(-0.5 * pre_act * pre_act) * inv_root_two_pi
    return cumulative + pre_act * density

def rotary_tables(segment_ids):
    token_count = segment_ids.shape[0]
    indices = jnp.arange(token_count, dtype=jnp.int32)
    earlier = jnp.concatenate([segment_ids[:1] - 1, segment_ids[:-1]])
    starts = lax.cummax(jnp.where(segment_ids != earlier, indices, 0), axis=0)
    places = (indices - starts).astype(jnp.float32)
    halves = jnp.arange(ROT // 2, dtype=jnp.float32)
    frequency = jnp.exp(halves * (-2.0 * math.log(10000.0) / ROT))
    angle_rows = places[:, None] * frequency[None, :]
    return (jnp.cos(angle_rows), jnp.sin(angle_rows))

def rotate(tensor, cosine, sine_table):
    half_rot = ROT // 2
    first_half = tensor[..., :half_rot]
    second_half = tensor[..., half_rot:ROT]
    cos_rows = cosine[:, None, :]
    sin_rows = sine_table[:, None, :]
    return jnp.concatenate([first_half * cos_rows - second_half * sin_rows, second_half * cos_rows + first_half * sin_rows, tensor[..., ROT:]], axis=-1)

def block_scores(query_block, key_rows, query_segs, key_segs, block_start):
    block_rows = query_block.shape[1]
    scores = jnp.einsum('hqd,hkd->hqk', query_block.astype(jnp.float32), key_rows.astype(jnp.float32)) * HD ** (-0.5)
    key_index = jnp.arange(key_rows.shape[1], dtype=jnp.int32)
    query_index = block_start + jnp.arange(block_rows, dtype=jnp.int32)
    allowed = (query_segs[:, None] == key_segs[None, :]) & (key_index[None, :] <= query_index[:, None])
    return jnp.where(allowed[None], scores, masked_score)

def attend(queries, key_rows, value_rows, segment_ids):
    head_count, token_count, head_width = queries.shape
    block_rows = min(512, token_count)

    def one_block(number):
        block_start = number * block_rows
        query_block = lax.dynamic_slice_in_dim(queries, block_start, block_rows, 1)
        query_segs = lax.dynamic_slice_in_dim(segment_ids, block_start, block_rows, 0)
        scores = block_scores(query_block, key_rows, query_segs, segment_ids, block_start)
        highest = lax.optimization_barrier(jnp.max(scores, axis=-1, keepdims=True))
        exponent = jnp.exp(scores - highest)
        row_total = lax.optimization_barrier(jnp.sum(exponent, axis=-1, keepdims=True))
        weights = (exponent / row_total).astype(jnp.bfloat16)
        mixed_out = jnp.einsum('hqk,hkd->hqd', weights.astype(jnp.float32), value_rows.astype(jnp.float32)).astype(jnp.bfloat16)
        return (mixed_out, (highest + jnp.log(row_total))[..., 0])
    mixed_out, log_total = lax.map(one_block, jnp.arange(token_count // block_rows, dtype=jnp.int32))
    mixed_out = jnp.transpose(mixed_out, (1, 0, 2, 3)).reshape(head_count, token_count, head_width)
    log_total = jnp.transpose(log_total, (1, 0, 2)).reshape(head_count, token_count)
    return (mixed_out, log_total)

def attend_back(queries, key_rows, value_rows, segment_ids, log_total, grad_heads):
    head_count, token_count, head_width = queries.shape
    block_rows = min(512, token_count)

    def one_block(accum_pair, number):
        key_grad, value_grad = accum_pair
        block_start = number * block_rows
        query_block = lax.dynamic_slice_in_dim(queries, block_start, block_rows, 1)
        grad_block = lax.dynamic_slice_in_dim(grad_heads, block_start, block_rows, 1)
        query_segs = lax.dynamic_slice_in_dim(segment_ids, block_start, block_rows, 0)
        lse_block = lax.dynamic_slice_in_dim(log_total, block_start, block_rows, 1)
        scores = block_scores(query_block, key_rows, query_segs, segment_ids, block_start)
        prob_full = jnp.exp(scores - lse_block[..., None])
        prob_half = prob_full.astype(jnp.bfloat16)
        prob_grad = jnp.einsum('hqd,hkd->hqk', grad_block.astype(jnp.float32), value_rows.astype(jnp.float32))
        row_delta = lax.optimization_barrier(jnp.sum(prob_full * prob_grad, axis=-1, keepdims=True))
        score_grad = (prob_full * (prob_grad - row_delta) * HD ** (-0.5)).astype(jnp.bfloat16)
        query_grad = jnp.einsum('hqk,hkd->hqd', score_grad.astype(jnp.float32), key_rows.astype(jnp.float32))
        key_grad = key_grad + jnp.einsum('hqk,hqd->hkd', score_grad.astype(jnp.float32), query_block.astype(jnp.float32))
        value_grad = value_grad + jnp.einsum('hqk,hqd->hkd', prob_half.astype(jnp.float32), grad_block.astype(jnp.float32))
        return ((key_grad, value_grad), query_grad)
    start_zero = jnp.zeros((head_count, token_count, head_width), jnp.float32)
    (key_grad, value_grad), query_grad = lax.scan(one_block, (start_zero, start_zero), jnp.arange(token_count // block_rows, dtype=jnp.int32))
    query_grad = jnp.transpose(query_grad, (1, 0, 2, 3)).reshape(head_count, token_count, head_width)
    return (query_grad, key_grad, value_grad)

def layer_forward(rows_in, segment_ids, qkv_mat, out_mat, up_mat, down_mat, vector_row):
    token_count = rows_in.shape[0]
    rows_float = rows_in.astype(jnp.float32)
    normed, scaling = normalize(rows_float)
    first_in = (normed * vector_row[0:D] + vector_row[D:2 * D]).astype(jnp.bfloat16)
    second_in = (normed * vector_row[2 * D:3 * D] + vector_row[3 * D:4 * D]).astype(jnp.bfloat16)
    projected = jnp.dot(first_in, qkv_mat.reshape(D, 3 * D), preferred_element_type=jnp.float32).reshape(token_count, 3, D)
    cosine, sine_table = rotary_tables(segment_ids)
    queries = (projected[:, 0] + vector_row[4 * D:5 * D]).reshape(token_count, HEADS, HD)
    key_rows = (projected[:, 1] + vector_row[5 * D:6 * D]).reshape(token_count, HEADS, HD)
    value_rows = (projected[:, 2] + vector_row[6 * D:7 * D]).reshape(token_count, HEADS, HD)
    queries = jnp.transpose(rotate(queries, cosine, sine_table).astype(jnp.bfloat16), (1, 0, 2))
    key_rows = jnp.transpose(rotate(key_rows, cosine, sine_table).astype(jnp.bfloat16), (1, 0, 2))
    value_rows = jnp.transpose(value_rows.astype(jnp.bfloat16), (1, 0, 2))
    mixed_out, log_total = attend(queries, key_rows, value_rows, segment_ids)
    attn_rows = jnp.transpose(mixed_out, (1, 0, 2)).reshape(token_count, D)
    pre_act = jnp.dot(second_in, up_mat, preferred_element_type=jnp.float32) + vector_row[9 * D:]
    hidden = gelu_value(pre_act).astype(jnp.bfloat16)
    branch_sum = jnp.dot(attn_rows, out_mat, preferred_element_type=jnp.float32) + jnp.dot(hidden, down_mat, preferred_element_type=jnp.float32)
    result = (rows_float + branch_sum + vector_row[7 * D:8 * D] + vector_row[8 * D:9 * D]).astype(jnp.bfloat16)
    saved = (normed, scaling, first_in, second_in, queries, key_rows, value_rows, attn_rows, log_total, pre_act, hidden, cosine, sine_table)
    return (result, saved)

def layer_backward(saved, cot_rows, segment_ids, qkv_mat, out_mat, up_mat, down_mat, vector_row):
    normed, scaling, first_in, second_in, queries, key_rows, value_rows, attn_rows, log_total, pre_act, hidden, cosine, sine_table = saved
    token_count = cot_rows.shape[0]
    cot_float = cot_rows.astype(jnp.float32)
    pre_grad = jnp.dot(cot_rows, down_mat.T, preferred_element_type=jnp.float32) * gelu_slope(pre_act)
    pre_half = pre_grad.astype(jnp.bfloat16)
    second_grad = jnp.dot(pre_half, up_mat.T, preferred_element_type=jnp.float32)
    attn_grad = jnp.dot(cot_rows, out_mat.T, preferred_element_type=jnp.float32).astype(jnp.bfloat16)
    grad_heads = jnp.transpose(attn_grad.reshape(token_count, HEADS, HD), (1, 0, 2))
    query_grad, key_grad, value_grad = attend_back(queries, key_rows, value_rows, segment_ids, log_total, grad_heads)
    query_grad = rotate(jnp.transpose(query_grad, (1, 0, 2)), cosine, -sine_table).reshape(token_count, D)
    key_grad = rotate(jnp.transpose(key_grad, (1, 0, 2)), cosine, -sine_table).reshape(token_count, D)
    value_grad = jnp.transpose(value_grad, (1, 0, 2)).reshape(token_count, D)
    qkv_half = jnp.stack([query_grad, key_grad, value_grad], axis=1).astype(jnp.bfloat16).reshape(token_count, 3 * D)
    first_grad = jnp.dot(qkv_half, qkv_mat.reshape(D, 3 * D).T, preferred_element_type=jnp.float32)
    normed_grad = first_grad * vector_row[0:D] + second_grad * vector_row[2 * D:3 * D]
    centred = normed_grad - lax.optimization_barrier(jnp.mean(normed_grad, axis=-1, keepdims=True)) - normed * lax.optimization_barrier(jnp.mean(normed_grad * normed, axis=-1, keepdims=True))
    grad_rows = (cot_float + scaling * centred).astype(jnp.bfloat16)
    qkv_term = jnp.dot(first_in.T, qkv_half, preferred_element_type=jnp.float32).reshape(D, 3, D)
    out_term = jnp.dot(attn_rows.T, cot_rows, preferred_element_type=jnp.float32)
    up_term = jnp.dot(second_in.T, pre_half, preferred_element_type=jnp.float32)
    down_term = jnp.dot(hidden.T, cot_rows, preferred_element_type=jnp.float32)
    bias_sum = lax.optimization_barrier(jnp.sum(cot_float, axis=0))
    vector_term = jnp.concatenate([lax.optimization_barrier(jnp.sum(first_grad * normed, axis=0)), lax.optimization_barrier(jnp.sum(first_grad, axis=0)), lax.optimization_barrier(jnp.sum(second_grad * normed, axis=0)), lax.optimization_barrier(jnp.sum(second_grad, axis=0)), lax.optimization_barrier(jnp.sum(query_grad, axis=0)), lax.optimization_barrier(jnp.sum(key_grad, axis=0)), lax.optimization_barrier(jnp.sum(value_grad, axis=0)), bias_sum, bias_sum, lax.optimization_barrier(jnp.sum(pre_grad, axis=0))])
    return (grad_rows, (qkv_term, out_term, up_term, down_term, vector_term))

def reference(block_input, out_cotangent, segments, qkv_weight, out_weight, up_weight, down_weight, vectors):

    def forward_all(section, inputs_all):

        def one_seq(carry, item):
            rows_in, segment_ids = item
            result, saved = layer_forward(rows_in, segment_ids, qkv_weight[section], out_weight[section], up_weight[section], down_weight[section], vectors[section])
            return (carry, result)
        _, results = lax.scan(one_seq, jnp.zeros((), jnp.float32), (inputs_all, segments))
        return results

    def backward_all(section, inputs_all, cots_all):
        initial = (jnp.zeros((D, 3, D), jnp.float32), jnp.zeros((D, D), jnp.float32), jnp.zeros((D, FF), jnp.float32), jnp.zeros((FF, D), jnp.float32), jnp.zeros((9 * D + FF,), jnp.float32))

        def one_seq(accum, item):
            rows_in, segment_ids, cot_rows = item
            result, saved = layer_forward(rows_in, segment_ids, qkv_weight[section], out_weight[section], up_weight[section], down_weight[section], vectors[section])
            grad_rows, terms = layer_backward(saved, cot_rows, segment_ids, qkv_weight[section], out_weight[section], up_weight[section], down_weight[section], vectors[section])
            return (tuple((total_now + term_now for total_now, term_now in zip(accum, terms))), grad_rows)
        totals, grad_all = lax.scan(one_seq, initial, (inputs_all, segments, cots_all))
        return (grad_all, totals)
    first_out = forward_all(0, block_input)
    second_out = forward_all(1, first_out)
    second_grad, second_totals = backward_all(1, first_out, out_cotangent)
    first_grad, first_totals = backward_all(0, block_input, second_grad)
    return (jnp.stack([first_out, second_out]), jnp.stack([first_grad, second_grad]), jnp.stack([first_totals[0], second_totals[0]]), jnp.stack([first_totals[1], second_totals[1]]), jnp.stack([first_totals[2], second_totals[2]]), jnp.stack([first_totals[3], second_totals[3]]), jnp.stack([first_totals[4], second_totals[4]]))
```

```python
import math

import jax
import jax.numpy as jnp
from jax import lax
from jax.sharding import PartitionSpec as P

HD = 64
ROT = 16


epsilon = 1e-05
inv_root_two = 0.7071067811865476
inv_root_two_pi = 0.3989422804014327
masked_score = -1e30
line_most = 8


def from_behind(value, axis, steps):
    count = lax.axis_size(axis)
    first, last = (max(0, -steps), min(count, count - steps))
    return lax.ppermute(value, axis, [(source, source + steps) for source in range(first, last)])


def line_gather(shard, axis):
    count = lax.axis_size(axis)
    if count > line_most:
        return lax.all_gather(shard, axis, axis=0, tiled=True)
    rows = shard.shape[0]
    place = lax.axis_index(axis)
    from_left, from_right = {}, {}
    right_going = left_going = shard
    for step in range(1, count):
        right_going = lax.ppermute(
            right_going, axis, [(i, i + 1) for i in range(step - 1, count - 1)]
        )
        left_going = lax.ppermute(
            left_going, axis, [(i, i - 1) for i in range(1, count - step + 1)]
        )
        from_left[step] = right_going
        from_right[step] = left_going
    whole = jnp.zeros((count * rows,) + shard.shape[1:], shard.dtype)
    whole = lax.dynamic_update_slice_in_dim(whole, shard, place * rows, 0)
    for step in range(1, count):
        piece = jnp.where(place + step < count, from_right[step], from_left[count - step])
        whole = lax.dynamic_update_slice_in_dim(
            whole, piece, lax.rem(place + step, count) * rows, 0
        )
    return whole


def line_scatter(terms, axis):
    count = lax.axis_size(axis)
    if count > line_most:
        return lax.psum_scatter(
            terms.astype(jnp.bfloat16), axis, scatter_dimension=0, tiled=True
        ).astype(jnp.float32)
    rows = terms.shape[0] // count
    place = lax.axis_index(axis)

    def chunk(number):
        number = jnp.clip(number, 0, count - 1)
        return lax.dynamic_slice_in_dim(terms, number * rows, rows, 0)

    right_sum = left_sum = None
    for step in range(1, count):
        right_part = chunk(count - step + place)
        left_part = chunk(place - count + step)
        if right_sum is not None:
            right_part = right_part + right_sum
            left_part = left_part + left_sum
        right_sum = lax.ppermute(
            right_part.astype(jnp.bfloat16), axis, [(i, i + 1) for i in range(step)]
        ).astype(jnp.float32)
        left_sum = lax.ppermute(
            left_part.astype(jnp.bfloat16),
            axis,
            [(i, i - 1) for i in range(count - step, count)],
        ).astype(jnp.float32)
    total = chunk(place)
    if right_sum is not None:
        total = total + right_sum + left_sum
    return total


def halving_scatter(terms, axis):
    count = lax.axis_size(axis)
    if count & (count - 1):
        return lax.psum_scatter(
            terms.astype(jnp.bfloat16), axis, scatter_dimension=0, tiled=True
        ).astype(jnp.float32)
    place = lax.axis_index(axis)
    rows = terms.shape[0] // count
    held = terms.reshape((count, rows) + terms.shape[1:])
    stride = 1
    while stride < count:
        groups = held.shape[0] // 2
        split = held.reshape((groups, 2) + held.shape[1:])
        bit = lax.rem(place // stride, 2)
        keep = lax.dynamic_index_in_dim(split, bit, 1, keepdims=False)
        away = lax.dynamic_index_in_dim(split, 1 - bit, 1, keepdims=False)
        came = lax.ppermute(
            away.astype(jnp.bfloat16), axis, [(i, i ^ stride) for i in range(count)]
        )
        held = keep + came.astype(jnp.float32)
        stride *= 2
    return held[0]


def swap_gather(piece, axis):
    count = lax.axis_size(axis)
    if count > line_most:
        return lax.all_gather(piece, axis, axis=0)
    place = lax.axis_index(axis)
    whole = jnp.zeros((count,) + piece.shape, piece.dtype)
    whole = lax.dynamic_update_index_in_dim(whole, piece, place, 0)
    for step in range(1, count):
        came = lax.ppermute(piece, axis, [(i, (i + step) % count) for i in range(count)])
        whole = lax.dynamic_update_index_in_dim(
            whole, came, lax.rem(place - step + count, count), 0
        )
    return whole


def swap_scatter(terms, axis):
    count = lax.axis_size(axis)
    if count > line_most:
        return lax.psum_scatter(terms, axis, scatter_dimension=0, tiled=False)
    place = lax.axis_index(axis)
    total = lax.dynamic_index_in_dim(terms, place, 0, keepdims=False)
    for step in range(1, count):
        away = lax.dynamic_index_in_dim(terms, lax.rem(place + step, count), 0, keepdims=False)
        total = total + lax.ppermute(away, axis, [(i, (i + step) % count) for i in range(count)])
    return total


def normalize(values):
    average = jnp.mean(values, axis=-1, keepdims=True)
    centered = values - average
    variance = jnp.mean(centered * centered, axis=-1, keepdims=True)
    scaling = lax.rsqrt(variance + epsilon)
    return (centered * scaling, scaling)


def gelu_value(pre_act):
    return pre_act * (0.5 * (1.0 + lax.erf(pre_act * inv_root_two)))


def gelu_slope(pre_act):
    cumulative = 0.5 * (1.0 + lax.erf(pre_act * inv_root_two))
    density = jnp.exp(-0.5 * pre_act * pre_act) * inv_root_two_pi
    return cumulative + pre_act * density


def rotary_tables(segment_ids):
    token_count = segment_ids.shape[0]
    indices = jnp.arange(token_count, dtype=jnp.int32)
    earlier = jnp.concatenate([segment_ids[:1] - 1, segment_ids[:-1]])
    starts = lax.cummax(jnp.where(segment_ids != earlier, indices, 0), axis=0)
    places = (indices - starts).astype(jnp.float32)
    halves = jnp.arange(ROT // 2, dtype=jnp.float32)
    frequency = jnp.exp(halves * (-2.0 * math.log(10000.0) / ROT))
    angle_rows = places[:, None] * frequency[None, :]
    return (jnp.cos(angle_rows), jnp.sin(angle_rows))


def rotate(tensor, cosine, sine_table):
    half_rot = ROT // 2
    first_half = tensor[..., :half_rot]
    second_half = tensor[..., half_rot:ROT]
    cos_rows = cosine[:, None, :]
    sin_rows = sine_table[:, None, :]
    return jnp.concatenate(
        [
            first_half * cos_rows - second_half * sin_rows,
            second_half * cos_rows + first_half * sin_rows,
            tensor[..., ROT:],
        ],
        axis=-1,
    )


def masked_scores(queries, key_rows, segment_ids):
    scores = jnp.einsum(
        "hqd,hkd->hqk", queries, key_rows, preferred_element_type=jnp.float32
    ) * HD ** (-0.5)
    index = jnp.arange(key_rows.shape[1], dtype=jnp.int32)
    allowed = (segment_ids[:, None] == segment_ids[None, :]) & (index[None, :] <= index[:, None])
    return jnp.where(allowed[None], scores, masked_score)


def attend(queries, key_rows, value_rows, segment_ids):
    scores = masked_scores(queries, key_rows, segment_ids)
    highest = jnp.max(scores, axis=-1, keepdims=True)
    exponent = jnp.exp(scores - highest)
    row_total = jnp.sum(exponent, axis=-1, keepdims=True)
    weights = (exponent / row_total).astype(jnp.bfloat16)
    mixed_out = jnp.einsum(
        "hqk,hkd->hqd", weights, value_rows, preferred_element_type=jnp.float32
    ).astype(jnp.bfloat16)
    return (mixed_out, (highest + jnp.log(row_total))[..., 0])


def attend_back(queries, key_rows, value_rows, segment_ids, log_total, grad_heads):
    scores = masked_scores(queries, key_rows, segment_ids)
    prob_full = jnp.exp(scores - log_total[..., None])
    prob_half = prob_full.astype(jnp.bfloat16)
    prob_grad = jnp.einsum(
        "hqd,hkd->hqk", grad_heads, value_rows, preferred_element_type=jnp.float32
    )
    row_delta = jnp.sum(prob_full * prob_grad, axis=-1, keepdims=True)
    score_grad = (prob_full * (prob_grad - row_delta) * HD ** (-0.5)).astype(jnp.bfloat16)
    query_grad = jnp.einsum(
        "hqk,hkd->hqd", score_grad, key_rows, preferred_element_type=jnp.float32
    )
    key_grad = jnp.einsum("hqk,hqd->hkd", score_grad, queries, preferred_element_type=jnp.float32)
    value_grad = jnp.einsum(
        "hqk,hqd->hkd", prob_half, grad_heads, preferred_element_type=jnp.float32
    )
    return (query_grad, key_grad, value_grad)


def dot_nn(left, right):
    return jnp.dot(left, right, preferred_element_type=jnp.float32)


def dot_nt(left, right):
    return lax.dot_general(
        left, right, (((1,), (1,)), ((), ())), preferred_element_type=jnp.float32
    )


def dot_tn(left, right):
    return lax.dot_general(
        left, right, (((0,), (0,)), ((), ())), preferred_element_type=jnp.float32
    )


def per_device(
    block_input, out_cotangent, segments, qkv_weight, out_weight, up_weight, down_weight, vectors
):
    model = block_input.shape[2]
    local_width = qkv_weight.shape[3]
    ff_local = up_weight.shape[2]
    segment_ids = segments[0]
    token_count = segment_ids.shape[0]
    head_local = local_width // HD
    mp_count = lax.axis_size("mp")
    dp_count = lax.axis_size("dp")
    model_part = lax.axis_index("mp")
    section_index = lax.axis_index("section")
    input_rows = block_input[0]
    cot_given = out_cotangent[0]

    attn_shard = jnp.concatenate(
        [qkv_weight[0].reshape(-1, 3 * local_width), out_weight[0].T], axis=1
    )
    attn_full = line_gather(attn_shard, "dp")
    up_full = line_gather(up_weight[0], "dp")
    down_t = line_gather(down_weight[0].T, "dp")
    qkv_flat = attn_full[:, : 3 * local_width]
    out_t = attn_full[:, 3 * local_width :]

    own_vector = swap_gather(vectors[0], "dp")
    vector_full = jnp.transpose(swap_gather(own_vector, "mp"), (1, 0, 2)).reshape(-1)
    gain_first = vector_full[0:model]
    shift_first = vector_full[model : 2 * model]
    gain_second = vector_full[2 * model : 3 * model]
    shift_second = vector_full[3 * model : 4 * model]
    out_bias = vector_full[7 * model : 8 * model]
    down_bias = vector_full[8 * model : 9 * model]

    def bias_part(start, width):
        return lax.dynamic_slice_in_dim(vector_full, start + model_part * width, width)

    query_bias = bias_part(4 * model, local_width)
    key_bias = bias_part(5 * model, local_width)
    value_bias = bias_part(6 * model, local_width)
    up_bias = bias_part(9 * model, ff_local)
    cosine, sine_table = rotary_tables(segment_ids)

    def forward(rows_in):
        rows_all = lax.all_gather(rows_in, "mp", axis=0, tiled=True).astype(jnp.float32)
        normed, scaling = normalize(rows_all)
        first_in = (normed * gain_first + shift_first).astype(jnp.bfloat16)
        second_in = (normed * gain_second + shift_second).astype(jnp.bfloat16)
        projected = dot_nn(first_in, qkv_flat).reshape(token_count, 3, local_width)
        queries = (projected[:, 0] + query_bias).reshape(token_count, head_local, HD)
        key_rows = (projected[:, 1] + key_bias).reshape(token_count, head_local, HD)
        value_rows = (projected[:, 2] + value_bias).reshape(token_count, head_local, HD)
        queries = jnp.transpose(rotate(queries, cosine, sine_table).astype(jnp.bfloat16), (1, 0, 2))
        key_rows = jnp.transpose(
            rotate(key_rows, cosine, sine_table).astype(jnp.bfloat16), (1, 0, 2)
        )
        value_rows = jnp.transpose(value_rows.astype(jnp.bfloat16), (1, 0, 2))
        mixed_out, log_total = attend(queries, key_rows, value_rows, segment_ids)
        attn_rows = jnp.transpose(mixed_out, (1, 0, 2)).reshape(token_count, local_width)
        pre_act = dot_nn(second_in, up_full) + up_bias
        hidden = gelu_value(pre_act).astype(jnp.bfloat16)
        branch_sum = halving_scatter(dot_nt(attn_rows, out_t) + dot_nt(hidden, down_t), "mp")
        result = (rows_in.astype(jnp.float32) + branch_sum + out_bias + down_bias).astype(
            jnp.bfloat16
        )
        return (
            result,
            (
                rows_in,
                normed,
                first_in,
                second_in,
                queries,
                key_rows,
                value_rows,
                attn_rows,
                log_total,
                pre_act,
                hidden,
            ),
        )

    def backward(saved, cot_rows, with_weights):
        (
            rows_in,
            normed_all,
            first_in,
            second_in,
            queries,
            key_rows,
            value_rows,
            attn_rows,
            log_total,
            pre_act,
            hidden,
        ) = saved
        cot_all = lax.all_gather(cot_rows, "mp", axis=0, tiled=True)
        pre_grad = dot_nn(cot_all, down_t) * gelu_slope(pre_act)
        pre_half = pre_grad.astype(jnp.bfloat16)
        second_grad = dot_nt(pre_half, up_full)
        if with_weights:
            down_piece = line_scatter(dot_tn(cot_all, hidden), "dp")
            up_piece = line_scatter(dot_tn(second_in, pre_half), "dp")
        attn_grad = dot_nn(cot_all, out_t).astype(jnp.bfloat16)
        grad_heads = jnp.transpose(attn_grad.reshape(token_count, head_local, HD), (1, 0, 2))
        query_grad, key_grad, value_grad = attend_back(
            queries, key_rows, value_rows, segment_ids, log_total, grad_heads
        )
        query_grad = rotate(jnp.transpose(query_grad, (1, 0, 2)), cosine, -sine_table).reshape(
            token_count, local_width
        )
        key_grad = rotate(jnp.transpose(key_grad, (1, 0, 2)), cosine, -sine_table).reshape(
            token_count, local_width
        )
        value_grad = jnp.transpose(value_grad, (1, 0, 2)).reshape(token_count, local_width)
        qkv_half = jnp.concatenate([query_grad, key_grad, value_grad], axis=1).astype(jnp.bfloat16)
        first_grad = dot_nt(qkv_half, qkv_flat)
        normed, scaling = normalize(rows_in.astype(jnp.float32))
        normed_grad = halving_scatter(
            first_grad * gain_first + second_grad * gain_second, "mp"
        )
        centred = (
            normed_grad
            - jnp.mean(normed_grad, axis=-1, keepdims=True)
            - normed * jnp.mean(normed_grad * normed, axis=-1, keepdims=True)
        )
        cot_float = cot_rows.astype(jnp.float32)
        grad_rows = (cot_float + scaling * centred).astype(jnp.bfloat16)
        if not with_weights:
            return (grad_rows, None)
        attn_piece = line_scatter(
            jnp.concatenate([dot_tn(first_in, qkv_half), dot_tn(cot_all, attn_rows)], axis=1), "dp"
        )
        bias_sum = jnp.sum(cot_float, axis=0)
        vector_term = jnp.concatenate(
            [
                jnp.sum(first_grad * normed_all, axis=0),
                jnp.sum(first_grad, axis=0),
                jnp.sum(second_grad * normed_all, axis=0),
                jnp.sum(second_grad, axis=0),
                jnp.zeros((3 * model,), jnp.float32),
                bias_sum,
                bias_sum,
                jnp.zeros((ff_local * mp_count,), jnp.float32),
            ]
        )
        for start, values in (
            (4 * model, query_grad),
            (5 * model, key_grad),
            (6 * model, value_grad),
            (9 * model, pre_grad),
        ):
            vector_term = lax.dynamic_update_slice_in_dim(
                vector_term,
                jnp.sum(values, axis=0),
                start + model_part * values.shape[1],
                0,
            )
        vector_term = vector_term.reshape(dp_count, mp_count, -1)
        vector_piece = swap_scatter(
            swap_scatter(jnp.transpose(vector_term, (1, 0, 2)), "mp"), "dp"
        )
        qkv_piece = attn_piece[:, : 3 * local_width].reshape(-1, 3, local_width)
        out_piece = attn_piece[:, 3 * local_width :].T
        return (grad_rows, (qkv_piece, out_piece, up_piece, down_piece.T, vector_piece))

    first_out, unused_saved = forward(input_rows)
    passed = from_behind(first_out, "section", 1)
    section_in = jnp.where(section_index == 1, passed, input_rows)
    layer_rows, saved = forward(section_in)
    early_grad, unused_terms = backward(saved, cot_given, False)
    returned = from_behind(early_grad, "section", -1)
    section_cot = jnp.where(section_index == 0, returned, cot_given)
    grad_rows, pieces = backward(saved, section_cot, True)
    qkv_piece, out_piece, up_piece, down_piece, vector_piece = pieces
    return (
        layer_rows[None, None],
        grad_rows[None, None],
        qkv_piece[None],
        out_piece[None],
        up_piece[None],
        down_piece[None],
        vector_piece[None],
    )


def solution(mesh):
    return jax.shard_map(
        per_device,
        mesh=mesh,
        in_specs=(
            P("dp", "mp", None),
            P("dp", "mp", None),
            P("dp", None),
            P("section", "dp", None, "mp"),
            P("section", "mp", "dp"),
            P("section", "dp", "mp"),
            P("section", "mp", "dp"),
            P("section", ("dp", "mp")),
        ),
        out_specs=(
            P("section", "dp", "mp", None),
            P("section", "dp", "mp", None),
            P("section", "dp", None, "mp"),
            P("section", "mp", "dp"),
            P("section", "dp", "mp"),
            P("section", "mp", "dp"),
            P("section", ("dp", "mp")),
        ),
        check_vma=False,
    )
```

```python
import math

import jax
import jax.numpy as jnp
import numpy as np
from jax import lax
from jax.experimental import pallas as pl
from jax.experimental.pallas import tpu as pltpu
from jax.sharding import PartitionSpec as P

HD = 64
ROT = 16
SPAN = 128


epsilon = 1e-05
inv_root_two = 0.7071067811865476
inv_root_two_pi = 0.3989422804014327
masked_score = -1e30
line_most = 8
INTERPRET = False


def from_behind(value, axis, steps):
    count = lax.axis_size(axis)
    first, last = (max(0, -steps), min(count, count - steps))
    return lax.ppermute(value, axis, [(source, source + steps) for source in range(first, last)])


def dot_nn(left, right):
    return jnp.dot(left, right, preferred_element_type=jnp.float32)


def dot_nt(left, right):
    return lax.dot_general(
        left, right, (((1,), (1,)), ((), ())), preferred_element_type=jnp.float32
    )


def dot_tn(left, right):
    return lax.dot_general(
        left, right, (((0,), (0,)), ((), ())), preferred_element_type=jnp.float32
    )


def swap_matrix(width):
    row = np.arange(width)[:, None]
    column = np.arange(width)[None, :]
    inside = column % HD
    partner = np.where(inside < ROT // 2, column + ROT // 2, column - ROT // 2)
    return ((row == partner) & (inside < ROT)).astype(np.float32)


def head_lanes(number, width):
    lane = lax.broadcasted_iota(jnp.int32, (1, width), 1)
    return (lane >= number * HD) & (lane < (number + 1) * HD)


def keep_head(values, number):
    return jnp.where(head_lanes(number, values.shape[1]), values, jnp.zeros_like(values))


def block_mask(seg_col, seg_row, key_start, query_start):
    keys, queries = seg_col.shape[0], seg_row.shape[1]
    key_index = key_start + lax.broadcasted_iota(jnp.int32, (keys, queries), 0)
    query_index = query_start + lax.broadcasted_iota(jnp.int32, (keys, queries), 1)
    return (seg_col == seg_row) & (key_index <= query_index)


def attn_fwd_kernel(
    rows_ref, norm_ref, bias_ref, swap_bias_ref, weight_ref, swap_ref, cos_ref, sin_ref,
    seg_col_ref, seg_row_ref,
    normed_ref, first_ref, second_ref, query_ref, key_ref, value_ref, mixed_ref, lse_ref,
):
    tokens, _ = rows_ref.shape
    width = query_ref.shape[1]
    step_rows = 64

    def norm_step(number, carry):
        rows = pl.ds(pl.multiple_of(number * step_rows, step_rows), step_rows)
        values = rows_ref[rows, :].astype(jnp.float32)
        average = jnp.mean(values, axis=1, keepdims=True)
        centered = values - average
        variance = jnp.mean(centered * centered, axis=1, keepdims=True)
        normed = centered * lax.rsqrt(variance + epsilon)
        normed_ref[rows, :] = normed.astype(jnp.bfloat16)
        first_ref[rows, :] = (normed * norm_ref[0:1, :] + norm_ref[1:2, :]).astype(jnp.bfloat16)
        second_ref[rows, :] = (normed * norm_ref[2:3, :] + norm_ref[3:4, :]).astype(jnp.bfloat16)
        return carry

    lax.fori_loop(0, tokens // step_rows, norm_step, 0)
    swapped_weight = dot_nn(weight_ref[:, : 2 * width], swap_ref[...]).astype(jnp.bfloat16)
    first = first_ref[...]
    projected = dot_nn(first, weight_ref[:, : 3 * width]) + bias_ref[...]
    swapped = dot_nn(first, swapped_weight) + swap_bias_ref[...]
    cosine, sine = cos_ref[...], sin_ref[...]
    query_ref[...] = (projected[:, :width] * cosine + swapped[:, :width] * sine).astype(jnp.bfloat16)
    key_ref[...] = (
        projected[:, width : 2 * width] * cosine + swapped[:, width:] * sine
    ).astype(jnp.bfloat16)
    value_ref[...] = projected[:, 2 * width :].astype(jnp.bfloat16)
    span = min(SPAN, tokens)
    for block in range(tokens // span):
        start = block * span
        low = max(0, start - span)
        keys = key_ref[low : start + span, :]
        values = value_ref[low : start + span, :]
        queries = query_ref[start : start + span, :]
        kept = block_mask(
            seg_col_ref[low : start + span, :], seg_row_ref[:, start : start + span], low, start
        )
        mixed = None
        for head in range(width // HD):
            scores = dot_nt(keys, keep_head(queries, head)) * HD ** (-0.5)
            scores = jnp.where(kept, scores, masked_score)
            highest = jnp.max(scores, axis=0, keepdims=True)
            exponent = jnp.exp(scores - highest)
            total = jnp.sum(exponent, axis=0, keepdims=True)
            weights = (exponent / total).astype(jnp.bfloat16)
            lse_ref[head : head + 1, start : start + span] = highest + jnp.log(total)
            part = dot_tn(weights, keep_head(values, head))
            mixed = part if mixed is None else mixed + part
        mixed_ref[start : start + span, :] = mixed.astype(jnp.bfloat16)


def split_store(values, bit, away_ref, keep_ref):
    rows = away_ref.shape[1]
    for number in range(2 * away_ref.shape[0]):
        part = values[number * rows : (number + 1) * rows, :].astype(jnp.bfloat16)

        @pl.when(bit == number % 2)
        def _():
            keep_ref[number // 2] = part

        @pl.when(bit != number % 2)
        def _():
            away_ref[number // 2] = part


def mlp_fwd_kernel(
    bit_ref, second_ref, mixed_ref, bias_ref, up_ref, down_ref, attn_ref,
    hidden_ref, slope_ref, away_ref, keep_ref, scratch_ref,
):
    tokens = second_ref.shape[0]
    width = mixed_ref.shape[1]
    scratch_ref[...] = dot_nn(second_ref[...], up_ref[...])
    step_rows = 32

    def act_step(number, carry):
        rows = pl.ds(pl.multiple_of(number * step_rows, step_rows), step_rows)
        pre_act = scratch_ref[rows, :] + bias_ref[...]
        cumulative = 0.5 * (1.0 + lax.erf(pre_act * inv_root_two))
        density = jnp.exp(-0.5 * pre_act * pre_act) * inv_root_two_pi
        hidden_ref[rows, :] = (pre_act * cumulative).astype(jnp.bfloat16)
        slope_ref[rows, :] = (cumulative + pre_act * density).astype(jnp.bfloat16)
        return carry

    lax.fori_loop(0, tokens // step_rows, act_step, 0)
    branch = dot_nt(hidden_ref[...], down_ref[...]) + dot_nt(
        mixed_ref[...], attn_ref[:, 3 * width :]
    )
    split_store(branch, bit_ref[0], away_ref, keep_ref)


def attn_bwd_core(
    cot, attn_ref, swap_ref, cos_ref, sin_ref, seg_col_ref, seg_row_ref,
    query_ref, key_ref, value_ref, lse_ref, query_acc, key_acc, value_acc, out_grad_ref,
):
    tokens, width = query_ref.shape
    out_grad_ref[...] = dot_nn(cot, attn_ref[:, 3 * width :]).astype(jnp.bfloat16)
    small_swap = swap_ref[:width, :width]
    query_swap = dot_nn(query_ref[...], small_swap).astype(jnp.bfloat16)
    key_swap = dot_nn(key_ref[...], small_swap).astype(jnp.bfloat16)
    span = min(SPAN, tokens)
    blocks = tokens // span
    key_parts = [[] for _ in range(blocks)]
    for block in range(blocks):
        start = block * span
        low = max(0, start - span)
        stop = start + span
        keys, values = key_ref[low:stop, :], value_ref[low:stop, :]
        queries, grads = query_ref[start:stop, :], out_grad_ref[start:stop, :]
        kept = block_mask(seg_col_ref[low:stop, :], seg_row_ref[:, start:stop], low, start)
        query_grad = query_turn = key_grad = key_turn = value_grad = None
        for head in range(width // HD):
            head_queries = keep_head(queries, head)
            head_grads = keep_head(grads, head)
            scores = dot_nt(keys, head_queries) * HD ** (-0.5)
            prob = jnp.where(
                kept, jnp.exp(scores - lse_ref[head : head + 1, start:stop]), 0.0
            )
            prob_grad = dot_nt(values, head_grads)
            delta = jnp.sum(prob * prob_grad, axis=0, keepdims=True)
            score_grad = (prob * (prob_grad - delta) * HD ** (-0.5)).astype(jnp.bfloat16)
            parts = (
                dot_tn(score_grad, keep_head(keys, head)),
                dot_tn(score_grad, keep_head(key_swap[low:stop, :], head)),
                dot_nn(score_grad, head_queries),
                dot_nn(score_grad, keep_head(query_swap[start:stop, :], head)),
                dot_nn(prob.astype(jnp.bfloat16), head_grads),
            )
            if head == 0:
                query_grad, query_turn, key_grad, key_turn, value_grad = parts
            else:
                query_grad, query_turn, key_grad, key_turn, value_grad = (
                    query_grad + parts[0],
                    query_turn + parts[1],
                    key_grad + parts[2],
                    key_turn + parts[3],
                    value_grad + parts[4],
                )
        query_acc[start:stop, :] = (
            query_grad * cos_ref[start:stop, :] - query_turn * sin_ref[start:stop, :]
        )
        key_back = key_grad * cos_ref[low:stop, :] - key_turn * sin_ref[low:stop, :]
        if block == 0:
            key_acc[start:stop, :] = key_back
            value_acc[start:stop, :] = value_grad
        else:
            key_acc[low:start, :] += key_back[:span]
            value_acc[low:start, :] += value_grad[:span]
            key_acc[start:stop, :] = key_back[span:]
            value_acc[start:stop, :] = value_grad[span:]


def first_grad_of(attn_ref, halves, width):
    total = None
    for number, half in enumerate(halves):
        part = dot_nt(half, attn_ref[:, number * width : (number + 1) * width])
        total = part if total is None else total + part
    return total


def bwd_kernel(
    bit_ref, cot_ref, slope_ref, norm_ref, attn_ref, up_ref, down_ref, swap_ref, cos_ref, sin_ref,
    seg_col_ref, seg_row_ref, query_ref, key_ref, value_ref, lse_ref,
    away_ref, keep_ref,
    query_acc, key_acc, value_acc, out_grad_ref,
):
    width = query_ref.shape[1]
    cot = cot_ref[...]
    attn_bwd_core(
        cot, attn_ref, swap_ref, cos_ref, sin_ref, seg_col_ref, seg_row_ref,
        query_ref, key_ref, value_ref, lse_ref, query_acc, key_acc, value_acc, out_grad_ref,
    )
    halves = [acc[...].astype(jnp.bfloat16) for acc in (query_acc, key_acc, value_acc)]
    pre_half = (dot_nn(cot, down_ref[...]) * slope_ref[...].astype(jnp.float32)).astype(
        jnp.bfloat16
    )
    normed_grad = first_grad_of(attn_ref, halves, width) * norm_ref[0:1, :] + dot_nt(
        pre_half, up_ref[...]
    ) * norm_ref[2:3, :]
    split_store(normed_grad, bit_ref[0], away_ref, keep_ref)


def column_sum(values):
    return jnp.sum(values, axis=0, keepdims=True)


def bwd_mlp_kernel(
    cot_ref, slope_ref, hidden_ref, second_ref, normed_ref, norm_ref, up_ref, down_ref,
    down_grad_ref, up_grad_ref, normed_grad_ref, sums_ref, up_sum_ref,
):
    cot = cot_ref[...]
    down_grad_ref[...] = dot_tn(cot, hidden_ref[...]).astype(jnp.bfloat16)
    pre_grad = dot_nn(cot, down_ref[...]) * slope_ref[...].astype(jnp.float32)
    up_sum_ref[...] = column_sum(pre_grad)
    pre_half = pre_grad.astype(jnp.bfloat16)
    up_grad_ref[...] = dot_tn(second_ref[...], pre_half).astype(jnp.bfloat16)
    second_grad = dot_nt(pre_half, up_ref[...])
    sums_ref[0:1, :] = column_sum(second_grad * normed_ref[...].astype(jnp.float32))
    sums_ref[1:2, :] = column_sum(second_grad)
    normed_grad_ref[...] = second_grad * norm_ref[2:3, :]


def bwd_attn_kernel(
    bit_ref, cot_ref, part_ref, first_ref, mixed_ref, normed_ref, norm_ref, attn_ref, swap_ref,
    cos_ref, sin_ref, seg_col_ref, seg_row_ref, query_ref, key_ref, value_ref, lse_ref,
    away_ref, keep_ref, attn_grad_ref, sums_ref, bias_sum_ref,
    query_acc, key_acc, value_acc, out_grad_ref,
):
    width = query_ref.shape[1]
    attn_bwd_core(
        cot_ref[...], attn_ref, swap_ref, cos_ref, sin_ref, seg_col_ref, seg_row_ref,
        query_ref, key_ref, value_ref, lse_ref, query_acc, key_acc, value_acc, out_grad_ref,
    )
    attn_grad_ref[:, 3 * width :] = dot_tn(cot_ref[...], mixed_ref[...]).astype(jnp.bfloat16)
    halves = []
    for number, acc in enumerate((query_acc, key_acc, value_acc)):
        values = acc[...]
        bias_sum_ref[number : number + 1, :] = column_sum(values)
        halves.append(values.astype(jnp.bfloat16))
        attn_grad_ref[:, number * width : (number + 1) * width] = dot_tn(
            first_ref[...], halves[-1]
        ).astype(jnp.bfloat16)
    first_grad = first_grad_of(attn_ref, halves, width)
    sums_ref[0:1, :] = column_sum(first_grad * normed_ref[...].astype(jnp.float32))
    sums_ref[1:2, :] = column_sum(first_grad)
    split_store(
        first_grad * norm_ref[0:1, :] + part_ref[...], bit_ref[0], away_ref, keep_ref
    )


def assemble_kernel(place_ref, *refs):
    pieces, whole_ref = refs[:-1], refs[-1]
    rows = pieces[0].shape[0]
    count = whole_ref.shape[0] // rows
    place = place_ref[0]
    whole_ref[pl.ds(pl.multiple_of(place * rows, 16), rows), :] = pieces[0][...]
    for step in range(1, count):
        left_ref, right_ref = pieces[2 * step - 1], pieces[2 * step]

        @pl.when(place >= step)
        def _():
            whole_ref[pl.ds(pl.multiple_of((place - step) * rows, 16), rows), :] = left_ref[...]

        @pl.when(place + step < count)
        def _():
            whole_ref[pl.ds(pl.multiple_of((place + step) * rows, 16), rows), :] = right_ref[...]


def call_kernel(body, name, inputs, outputs, scalars=0, scratch=()):
    vmem = pl.BlockSpec(memory_space=pltpu.VMEM)
    smem = pl.BlockSpec(memory_space=pltpu.SMEM)
    return pl.pallas_call(
        body,
        name=name,
        out_shape=[jax.ShapeDtypeStruct(shape, dtype) for shape, dtype in outputs],
        in_specs=[smem] * scalars + [vmem] * (len(inputs) - scalars),
        out_specs=[vmem] * len(outputs),
        scratch_shapes=[pltpu.VMEM(shape, dtype) for shape, dtype in scratch],
        interpret=INTERPRET,
    )(*inputs)


def line_pieces(shard, axis):
    count = lax.axis_size(axis)
    pieces = [shard]
    right_going = left_going = shard
    for step in range(1, count):
        right_going = lax.ppermute(
            right_going, axis, [(i, i + 1) for i in range(step - 1, count - 1)]
        )
        left_going = lax.ppermute(
            left_going, axis, [(i, i - 1) for i in range(1, count - step + 1)]
        )
        pieces += [right_going, left_going]
    return pieces


def line_gather(shard, axis):
    count = lax.axis_size(axis)
    if count > line_most:
        return lax.all_gather(shard, axis, axis=0, tiled=True)
    pieces = line_pieces(shard, axis)
    place = lax.axis_index(axis).astype(jnp.int32).reshape(1)
    (whole,) = call_kernel(
        assemble_kernel,
        "assemble",
        [place] + pieces,
        [((count * shard.shape[0], shard.shape[1]), shard.dtype)],
        scalars=1,
    )
    return whole


def line_scatter(terms, axis):
    count = lax.axis_size(axis)
    if count > line_most:
        return lax.psum_scatter(terms, axis, scatter_dimension=0, tiled=True).astype(jnp.float32)
    rows = terms.shape[0] // count
    place = lax.axis_index(axis)

    def chunk(number):
        number = jnp.clip(number, 0, count - 1)
        return lax.dynamic_slice_in_dim(terms, number * rows, rows, 0)

    def joined(part, came):
        return (part.astype(jnp.float32) + came.astype(jnp.float32)).astype(jnp.bfloat16)

    right_sum = left_sum = None
    for step in range(1, count):
        right_part = chunk(count - step + place)
        left_part = chunk(place - count + step)
        if right_sum is not None:
            right_part = joined(right_part, right_sum)
            left_part = joined(left_part, left_sum)
        right_sum = lax.ppermute(right_part, axis, [(i, i + 1) for i in range(step)])
        left_sum = lax.ppermute(
            left_part, axis, [(i, i - 1) for i in range(count - step, count)]
        )
    total = chunk(place).astype(jnp.float32)
    if right_sum is not None:
        total = total + right_sum.astype(jnp.float32) + left_sum.astype(jnp.float32)
    return total


def halving_scatter(away, keep, axis):
    count = lax.axis_size(axis)
    place = lax.axis_index(axis)
    stride = 1
    while True:
        came = lax.ppermute(away, axis, [(i, i ^ stride) for i in range(count)])
        held = keep.astype(jnp.float32) + came.astype(jnp.float32)
        stride *= 2
        if stride == count:
            return held[0]
        split = held.reshape((held.shape[0] // 2, 2) + held.shape[1:])
        bit = lax.rem(place // stride, 2)
        keep = lax.dynamic_index_in_dim(split, bit, 1, keepdims=False)
        away = lax.dynamic_index_in_dim(split, 1 - bit, 1, keepdims=False).astype(jnp.bfloat16)


def swap_gather(piece, axis):
    count = lax.axis_size(axis)
    if count > line_most:
        return lax.all_gather(piece, axis, axis=0)
    place = lax.axis_index(axis)
    whole = jnp.zeros((count,) + piece.shape, piece.dtype)
    whole = lax.dynamic_update_index_in_dim(whole, piece, place, 0)
    for step in range(1, count):
        came = lax.ppermute(piece, axis, [(i, (i + step) % count) for i in range(count)])
        whole = lax.dynamic_update_index_in_dim(
            whole, came, lax.rem(place - step + count, count), 0
        )
    return whole


def swap_scatter(terms, axis):
    count = lax.axis_size(axis)
    if count > line_most:
        return lax.psum_scatter(terms, axis, scatter_dimension=0, tiled=False)
    place = lax.axis_index(axis)
    total = lax.dynamic_index_in_dim(terms, place, 0, keepdims=False)
    for step in range(1, count):
        away = lax.dynamic_index_in_dim(terms, lax.rem(place + step, count), 0, keepdims=False)
        total = total + lax.ppermute(away, axis, [(i, (i + step) % count) for i in range(count)])
    return total


def normalize(values):
    average = jnp.mean(values, axis=-1, keepdims=True)
    centered = values - average
    variance = jnp.mean(centered * centered, axis=-1, keepdims=True)
    scaling = lax.rsqrt(variance + epsilon)
    return (centered * scaling, scaling)


def rotary_tables(segment_ids, width):
    token_count = segment_ids.shape[0]
    indices = jnp.arange(token_count, dtype=jnp.int32)
    earlier = jnp.concatenate([segment_ids[:1] - 1, segment_ids[:-1]])
    starts = lax.cummax(jnp.where(segment_ids != earlier, indices, 0), axis=0)
    places = (indices - starts).astype(jnp.float32)
    inside = jnp.arange(width, dtype=jnp.int32) % HD
    halves = (inside % (ROT // 2)).astype(jnp.float32)
    frequency = jnp.exp(halves * (-2.0 * math.log(10000.0) / ROT))
    angle_rows = places[:, None] * frequency[None, :]
    sign = jnp.where(inside < ROT // 2, -1.0, 1.0)
    turned = (inside < ROT)[None, :]
    return (
        jnp.where(turned, jnp.cos(angle_rows), 1.0),
        jnp.where(turned, jnp.sin(angle_rows) * sign[None, :], 0.0),
    )


def per_device(
    block_input, out_cotangent, segments, qkv_weight, out_weight, up_weight, down_weight, vectors
):
    model = block_input.shape[2]
    width = qkv_weight.shape[3]
    hidden_width = up_weight.shape[2]
    segment_ids = segments[0]
    tokens = segment_ids.shape[0]
    mp_count = lax.axis_size("mp")
    dp_count = lax.axis_size("dp")
    own_rows = tokens // mp_count
    model_part = lax.axis_index("mp")
    section_index = lax.axis_index("section")
    low_bit = lax.rem(model_part, 2).astype(jnp.int32).reshape(1)
    input_rows = block_input[0]
    cot_given = out_cotangent[0]
    bf16, f32 = jnp.bfloat16, jnp.float32

    attn_shard = jnp.concatenate([qkv_weight[0].reshape(-1, 3 * width), out_weight[0].T], axis=1)
    attn_full = line_gather(attn_shard, "dp")
    up_full = line_gather(up_weight[0], "dp")
    down_t = line_gather(down_weight[0].T, "dp")

    vector_full = jnp.transpose(
        swap_gather(swap_gather(vectors[0], "dp"), "mp"), (1, 0, 2)
    ).reshape(-1)
    norm_rows = vector_full[: 4 * model].reshape(4, model)
    added_bias = vector_full[7 * model : 8 * model] + vector_full[8 * model : 9 * model]

    def bias_part(start, wide):
        return lax.dynamic_slice_in_dim(vector_full, start + model_part * wide, wide)

    qkv_bias = jnp.concatenate([bias_part(n * model, width) for n in (4, 5, 6)])
    heads = qkv_bias[: 2 * width].reshape(-1, HD)
    half = ROT // 2
    swap_bias = jnp.concatenate(
        [heads[:, half:ROT], heads[:, :half], jnp.zeros_like(heads[:, ROT:])], axis=1
    ).reshape(1, 2 * width)
    qkv_bias = qkv_bias.reshape(1, 3 * width)
    up_bias = bias_part(9 * model, hidden_width).reshape(1, hidden_width)
    cosine, sine = rotary_tables(segment_ids, width)
    seg_col, seg_row = segment_ids[:, None], segment_ids[None, :]
    swap = jnp.asarray(swap_matrix(2 * width), bf16)
    halved = ((mp_count // 2, own_rows, model), bf16)
    kept_heads = -(-(width // HD) // 8) * 8

    def forward(rows_in):
        rows_all = lax.all_gather(rows_in, "mp", axis=0, tiled=True)
        normed, first, second, queries, keys, values, mixed, lse = call_kernel(
            attn_fwd_kernel,
            "attn_fwd",
            [rows_all, norm_rows, qkv_bias, swap_bias, attn_full, swap, cosine, sine]
            + [seg_col, seg_row],
            [((tokens, model), bf16)] * 3 + [((tokens, width), bf16)] * 4
            + [((kept_heads, tokens), f32)],
        )
        hidden, slope, away, keep = call_kernel(
            mlp_fwd_kernel,
            "mlp_fwd",
            [low_bit, second, mixed, up_bias, up_full, down_t, attn_full],
            [((tokens, hidden_width), bf16)] * 2 + [halved] * 2,
            scalars=1,
            scratch=[((tokens, hidden_width), f32)],
        )
        branch_sum = halving_scatter(away, keep, "mp")
        result = (rows_in.astype(f32) + branch_sum + added_bias).astype(bf16)
        return (
            result,
            (rows_in, normed, first, second, queries, keys, values, mixed, lse, hidden, slope),
        )

    def backward(saved, cot_rows, with_weights):
        rows_in, normed_all, first, second, queries, keys, values, mixed, lse, hidden, slope = saved
        cot_all = lax.all_gather(cot_rows, "mp", axis=0, tiled=True)
        attn_inputs = [attn_full, swap, cosine, sine, seg_col, seg_row, queries, keys, values, lse]
        attn_scratch = [((tokens, width), f32)] * 3 + [((tokens, width), bf16)]
        if not with_weights:
            away, keep = call_kernel(
                bwd_kernel,
                "bwd",
                [low_bit, cot_all, slope, norm_rows, attn_full, up_full, down_t]
                + attn_inputs[1:],
                [halved] * 2,
                scalars=1,
                scratch=attn_scratch,
            )
        else:
            down_grad, up_grad, part, second_sums, up_sum = call_kernel(
                bwd_mlp_kernel,
                "bwd_mlp",
                [cot_all, slope, hidden, second, normed_all, norm_rows, up_full, down_t],
                [((model, hidden_width), bf16)] * 2
                + [((tokens, model), f32), ((2, model), f32), ((1, hidden_width), f32)],
            )
            down_piece = line_scatter(down_grad, "dp")
            up_piece = line_scatter(up_grad, "dp")
            away, keep, attn_grad, first_sums, bias_sums = call_kernel(
                bwd_attn_kernel,
                "bwd_attn",
                [low_bit, cot_all, part, first, mixed, normed_all, norm_rows] + attn_inputs,
                [halved] * 2
                + [((model, 4 * width), bf16), ((2, model), f32), ((3, width), f32)],
                scalars=1,
                scratch=attn_scratch,
            )
            attn_piece = line_scatter(attn_grad, "dp")
        normed, scaling = normalize(rows_in.astype(f32))
        normed_grad = halving_scatter(away, keep, "mp")
        centred = (
            normed_grad
            - jnp.mean(normed_grad, axis=-1, keepdims=True)
            - normed * jnp.mean(normed_grad * normed, axis=-1, keepdims=True)
        )
        cot_float = cot_rows.astype(f32)
        grad_rows = (cot_float + scaling * centred).astype(bf16)
        if not with_weights:
            return (grad_rows, None)
        is_mine = (jnp.arange(mp_count) == model_part)[:, None]
        bias_sum = jnp.sum(cot_float, axis=0)
        vector_term = jnp.concatenate(
            [first_sums.reshape(-1), second_sums.reshape(-1)]
            + [jnp.where(is_mine, bias_sums[n : n + 1], 0.0).reshape(-1) for n in range(3)]
            + [bias_sum, bias_sum, jnp.where(is_mine, up_sum, 0.0).reshape(-1)]
        ).reshape(dp_count, mp_count, -1)
        vector_piece = swap_scatter(
            swap_scatter(jnp.transpose(vector_term, (1, 0, 2)), "mp"), "dp"
        )
        qkv_piece = attn_piece[:, : 3 * width].reshape(-1, 3, width)
        out_piece = attn_piece[:, 3 * width :].T
        return (grad_rows, (qkv_piece, out_piece, up_piece, down_piece.T, vector_piece))

    first_out, unused_saved = forward(input_rows)
    passed = from_behind(first_out, "section", 1)
    section_in = jnp.where(section_index == 1, passed, input_rows)
    layer_rows, saved = forward(section_in)
    early_grad, unused_terms = backward(saved, cot_given, False)
    returned = from_behind(early_grad, "section", -1)
    section_cot = jnp.where(section_index == 0, returned, cot_given)
    grad_rows, pieces = backward(saved, section_cot, True)
    qkv_piece, out_piece, up_piece, down_piece, vector_piece = pieces
    return (
        layer_rows[None, None],
        grad_rows[None, None],
        qkv_piece[None],
        out_piece[None],
        up_piece[None],
        down_piece[None],
        vector_piece[None],
    )


def solution(mesh):
    return jax.shard_map(
        per_device,
        mesh=mesh,
        in_specs=(
            P("dp", "mp", None),
            P("dp", "mp", None),
            P("dp", None),
            P("section", "dp", None, "mp"),
            P("section", "mp", "dp"),
            P("section", "dp", "mp"),
            P("section", "mp", "dp"),
            P("section", ("dp", "mp")),
        ),
        out_specs=(
            P("section", "dp", "mp", None),
            P("section", "dp", "mp", None),
            P("section", "dp", None, "mp"),
            P("section", "mp", "dp"),
            P("section", "dp", "mp"),
            P("section", "mp", "dp"),
            P("section", ("dp", "mp")),
        ),
        check_vma=False,
    )
```
